32 devices in a mesh: fit: 8 (over z, x), col: 4 (over y, core).
Axes of the slice: x: 2, y: 2, z: 4, core: 2. Of those that a mesh axis runs over, the one named last changes fastest.
Arguments:
- trial: bfloat16 [8, 256, 512], P(None, 'fit', 'col'), may hold values from -6 to 6
- hole_factor: bfloat16 [256, 256, 256], P('fit'), may hold values from -0.03125 to 0.03125
- elec_factor: bfloat16 [256, 512, 512], P('fit', 'col'), may hold values from -0.25 to 0.25
- hole_energy: float32 [256], P('fit'), may hold values from -1.2 to -0.3
- elec_energy: float32 [512], P('col'), may hold values from 0.1 to 1.5
Outputs:
- applied: float32 [8, 256, 512], P(None, 'fit', 'col')
The draws below stay inside these ranges and needn't reach their ends.
All inputs are finite; a program needn't handle non-finite values.
Results may differ from the reference program's by a relative error of at most 0.0018.
Values may be sent and summed in bfloat16 or wider, within the bound.
No kernel may reach another device: no remote copies, remote signals or barrier semaphores. Data moves between devices by JAX's collectives and lax.ppermute only.
A program may use at most 64 MiB of HBM per device.

```python
import jax
import jax.numpy as jnp
from jax import lax

O = 256
V = 512
AUX_DEV = 32
NVEC = 8
NAUX = 256


def raised(drawn, rng, source, target, parts, factor):
    owner, partner = [(jnp.arange(drawn.shape[axis_at]) // (drawn.shape[axis_at] // parts)).reshape([-1 if axis == axis_at else 1 for axis in range(drawn.ndim)]) for axis_at in (source, target)]
    chosen = jax.random.permutation(rng, parts)[partner]
    strong = (owner == chosen) | (owner == (partner + parts // 2) % parts)
    return jnp.where(strong, factor * drawn, drawn)


def block_scale(own_key, extent, split, smallest, high):
    gain, own = 1.0, jax.random.fold_in(own_key, 6)
    for position, parts in split:
        steps = jnp.exp(jax.random.uniform(jax.random.fold_in(own, position), (parts,), jnp.float32, smallest / len(split), high / len(split)))
        gain = gain * jnp.repeat(steps, extent[position] // parts).reshape([-1 if axis == position else 1 for axis in range(len(extent))])
    return gain


def bell_draw(rng, shape, width, reach, split=(), dtype=jnp.bfloat16):
    drawn = jax.random.normal(rng, shape, jnp.float32) * width
    if len(split) > 0:
        drawn = block_scale(rng, shape, split, -0.22, 0.18) * drawn
    return jnp.clip(drawn, min=-reach, max=reach).astype(dtype)


def bell_draw_with(own_key, dims, scale, reach, cuts, heavy, held_as=jnp.bfloat16):
    array = scale * jax.random.normal(own_key, dims, jnp.float32)
    if cuts:
        array = array * block_scale(own_key, dims, cuts, -0.22, 0.18)
    return jnp.clip(raised(array, jax.random.fold_in(own_key, 3), *heavy), -reach, reach).astype(held_as)


def setup_inputs(seed: int = 0) -> dict:
    splits = jax.random.split(jax.random.key(seed), 6)
    return {
        "trial": bell_draw(splits[0], (NVEC, O, V), 1.0, 6.0, ((1, 8), (2, 4))),
        "hole_factor": bell_draw_with(splits[1], (NAUX, O, O), (O * NAUX) ** -0.5, 0.03125, ((0, 8),), (0, 1, 8, 2.0)),
        "elec_factor": bell_draw(splits[2], (NAUX, V, V), V ** -0.5, 0.25, ((0, 8), (1, 4))),
        "hole_energy": jnp.clip(-1.2 + 0.90000004 * jax.random.uniform(splits[3], (O,), jnp.float32) ** block_scale(splits[3], (O,), ((0, 8),), -0.2, 0.2), -1.2, -0.3),
        "elec_energy": jnp.clip(0.1 + 1.4 * jax.random.uniform(splits[4], (V,), jnp.float32) ** block_scale(splits[4], (V,), ((0, 4),), -0.2, 0.2), 0.1, 1.5),
    }


def reference(trial, hole_factor, elec_factor, hole_energy, elec_energy):
    block = 64 if NAUX % 64 == 0 else AUX_DEV
    count = NAUX // block
    hole_blocks = hole_factor.reshape(count, block, O, O)
    elec_blocks = elec_factor.reshape(count, block, V, V)
    trial_wide = trial.astype(jnp.float32)

    def step(total, pieces):
        hole_part, elec_part = pieces
        half = jnp.einsum("kjb,pab->kpja", trial_wide, elec_part.astype(jnp.float32)).astype(jnp.bfloat16)
        total = total + jnp.einsum("pij,kpja->kia", hole_part.astype(jnp.float32), half.astype(jnp.float32))
        return total, None

    direct, _ = lax.scan(step, jnp.zeros((NVEC, O, V), jnp.float32), (hole_blocks, elec_blocks))
    spread = elec_energy[None, :] - hole_energy[:, None]
    return direct + spread[None] * trial_wide
```

```python
import functools

import jax
import jax.numpy as jnp
from jax import lax
from jax.experimental import pallas as pl
from jax.experimental.pallas import tpu as pltpu
from jax.sharding import PartitionSpec as P

NT = (((1,), (1,)), ((), ()))


def dot(a, b):
    return lax.dot_general(a, b, NT, preferred_element_type=jnp.float32)


def digits_of(size):
    radices = []
    bits = size.bit_length() - 1
    if bits % 2:
        radices.append(2)
    return radices + [4] * (bits // 2)


def swap(value, axis, size, offset):
    return lax.ppermute(value, axis, [(at, at ^ offset) for at in range(size)])


def contract(fits, owners, block, where_ref, *refs):
    slabs = refs[: len(owners)]
    hole_ref, elec_ref = refs[len(owners) : len(owners) + 2]
    *outs, trial_ref, total_ref, turned_ref = refs[len(owners) + 2 :]
    fit, col = where_ref[0], where_ref[1]
    vectors, _, inner = trial_ref.shape
    rows, width = slabs[0].shape[2:]
    outer = elec_ref.shape[1]

    @pl.when(pl.program_id(0) == 0)
    def _():
        for slab, held in zip(slabs, owners):
            for at, (fit_off, col_off) in enumerate(held):
                row = pl.multiple_of((fit ^ fit_off) * rows, rows)
                column = pl.multiple_of((col ^ col_off) * width, width)
                trial_ref[:, pl.ds(row, rows), pl.ds(column, width)] = slab[at]
        total_ref[...] = jnp.zeros_like(total_ref)

    for vector in range(vectors):
        half = dot(elec_ref[...].reshape(block * outer, inner), trial_ref[vector]).astype(jnp.bfloat16)
        total = None
        for at in range(block):
            term = dot(half[at * outer : (at + 1) * outer], hole_ref[at])
            total = term if total is None else total + term
        total_ref[vector] += total

    @pl.when(pl.program_id(0) == pl.num_programs(0) - 1)
    def _():
        groups = len(outs)
        for vector in range(vectors):
            turned_ref[...] = total_ref[vector].T
            for offset in range(fits):
                row = pl.multiple_of((fit ^ offset) * rows, rows)
                out = outs[offset % groups]
                out[offset // groups, vector] = turned_ref[pl.ds(row, rows), :].astype(out.dtype)


def in_order(fits, cols, position, slabs, where):
    at = {owner: place for place, owner in enumerate(sum(where, []))}
    table = jnp.array([[at[f, c] for c in range(cols)] for f in range(fits)])
    chosen = table[(jnp.arange(fits) ^ position[0])[:, None], (jnp.arange(cols) ^ position[1])[None]]
    stack = jnp.concatenate(slabs)[chosen]
    _, _, vectors, rows, width = stack.shape
    return stack.transpose(2, 0, 3, 1, 4).reshape(1, vectors, fits * rows, cols * width)


def local(fits, cols, trial, hole_factor, elec_factor, hole_energy, elec_energy):
    vectors, rows, width = trial.shape
    count, outer, inner = elec_factor.shape
    holes = hole_factor.shape[1]
    radices = digits_of(fits)

    held, owners = trial[None], [(0, 0)]
    bit = cols // 2
    while bit > 1:
        held = jnp.concatenate([held, swap(held, "col", cols, bit)])
        owners = owners + [(f, c ^ bit) for f, c in owners]
        bit //= 2
    slabs, where = [], []
    stride = 1
    for place, radix in enumerate(radices):
        arrived = [held] + [swap(held, "fit", fits, step * stride) for step in range(1, radix)]
        named = [[(f ^ (step * stride), c) for f, c in owners] for step in range(radix)]
        if place < len(radices) - 1:
            held, owners = jnp.concatenate(arrived), sum(named, [])
        else:
            slabs, where = arrived, named
        stride *= radix
    if not radices:
        slabs, where = [held], [owners]
    if cols > 1:
        slabs, where = (
            slabs + [swap(slab, "col", cols, 1) for slab in slabs],
            where + [[(f, c ^ 1) for f, c in named] for named in where],
        )

    block = next(size for size in (8, 4, 2, 1) if count % size == 0)
    first = radices[0] if radices else 1
    position = jnp.stack([lax.axis_index("fit"), lax.axis_index("col")]).astype(jnp.int32)
    inside = rows % 16 == 0
    if inside:
        blocks, groups, places = fits, first, position
    else:
        blocks, groups, places = 1, 1, jnp.zeros_like(position)
        slabs, where = [in_order(fits, cols, position, slabs, where)], [[(0, 0)]]
    piece = (blocks // groups, vectors, holes // blocks, outer)
    kept, *sent = pl.pallas_call(
        functools.partial(contract, blocks, where, block),
        grid=(count // block,),
        in_specs=[pl.BlockSpec(memory_space=pltpu.SMEM)]
        + [pl.BlockSpec(slab.shape, lambda p: (0, 0, 0, 0)) for slab in slabs]
        + [
            pl.BlockSpec((block, holes, holes), lambda p: (p, 0, 0)),
            pl.BlockSpec((block, outer, inner), lambda p: (p, 0, 0)),
        ],
        out_specs=[pl.BlockSpec(piece, lambda p: (0, 0, 0, 0))] * groups,
        out_shape=[jax.ShapeDtypeStruct(piece, jnp.float32)]
        + [jax.ShapeDtypeStruct(piece, jnp.bfloat16)] * (groups - 1),
        scratch_shapes=[
            pltpu.VMEM((vectors, holes, inner), jnp.bfloat16),
            pltpu.VMEM((vectors, outer, holes), jnp.float32),
            pltpu.VMEM((holes, outer), jnp.float32),
        ],
        compiler_params=pltpu.CompilerParams(vmem_limit_bytes=40 << 20),
    )(places, *slabs, hole_factor, elec_factor)
    if not inside:
        pieces = kept.reshape(vectors, fits, rows, width).swapaxes(0, 1)
        pieces = pieces[jnp.arange(fits) ^ position[0]].reshape(fits // first, first, vectors, rows, width)
        kept = pieces[:, 0]
        sent = [pieces[:, step].astype(jnp.bfloat16) for step in range(1, first)]

    stride = 1
    for place, radix in enumerate(radices):
        for step in range(1, radix):
            kept = kept + swap(sent[step - 1], "fit", fits, step * stride).astype(jnp.float32)
        stride *= radix
        if place < len(radices) - 1:
            split = kept.reshape(kept.shape[0] // radices[place + 1], radices[place + 1], *kept.shape[1:])
            kept = split[:, 0]
            sent = [split[:, step].astype(jnp.bfloat16) for step in range(1, radices[place + 1])]
    spread = elec_energy[None, :] - hole_energy[:, None]
    return kept[0] + spread[None] * trial.astype(jnp.float32)


def solution(mesh):
    in_specs = (
        P(None, "fit", "col"),
        P("fit", None, None),
        P("fit", "col", None),
        P("fit"),
        P("col"),
    )
    body = functools.partial(local, mesh.shape["fit"], mesh.shape["col"])
    return jax.shard_map(body, mesh=mesh, in_specs=in_specs, out_specs=P(None, "fit", "col"), check_vma=False)
```

```python
import functools

import jax
import jax.numpy as jnp
from jax import lax
from jax.experimental import pallas as pl
from jax.experimental.pallas import tpu as pltpu
from jax.sharding import PartitionSpec as P


NT = (((1,), (1,)), ((), ()))


def dot(a, b):
    return lax.dot_general(a, b, NT, preferred_element_type=jnp.float32)


def digits_of(size):
    radices = []
    bits = size.bit_length() - 1
    if bits % 2:
        radices.append(2)
    return radices + [4] * (bits // 2)


def swap(value, axis, size, offset):
    return lax.ppermute(value, axis, [(at, at ^ offset) for at in range(size)])


def contract(fits, owners, where_ref, *refs):
    slabs = refs[: len(owners)]
    hole_ref, elec_ref = refs[len(owners) : len(owners) + 2]
    *outs, trial_ref, total_ref, turned_ref, holes_ref, elecs_ref, arrived = refs[len(owners) + 2 :]
    steps, block, outer, inner = elecs_ref.shape
    fit, col = where_ref[0], where_ref[1]
    vectors = trial_ref.shape[0]
    rows, width = slabs[0].shape[2:]

    def fetch(step, which):
        source, target = ((elec_ref, elecs_ref), (hole_ref, holes_ref))[which]
        return pltpu.make_async_copy(
            source.at[pl.ds(step * block, block)], target.at[step], arrived.at[which, step]
        )

    for step in range(steps):
        for which in range(2):
            fetch(step, which).start()
    for slab, held in zip(slabs, owners):
        for at, (fit_off, col_off) in enumerate(held):
            row = pl.multiple_of((fit ^ fit_off) * rows, rows)
            column = pl.multiple_of((col ^ col_off) * width, width)
            trial_ref[:, pl.ds(row, rows), pl.ds(column, width)] = slab[at]
    total_ref[...] = jnp.zeros_like(total_ref)

    @pl.loop(0, steps)
    def _(step):
        for which in range(2):
            fetch(step, which).wait()
        elec = elecs_ref.at[step]
        for vector in range(vectors):
            half = dot(elec[...].reshape(block * outer, inner), trial_ref[vector]).astype(jnp.bfloat16)
            total = None
            for at in range(block):
                term = dot(half[at * outer : (at + 1) * outer], holes_ref[step, at])
                total = term if total is None else total + term
            total_ref[vector] += total

    groups = len(outs)
    for vector in range(vectors):
        turned_ref[...] = total_ref[vector].T
        for offset in range(fits):
            row = pl.multiple_of((fit ^ offset) * rows, rows)
            out = outs[offset % groups]
            out[offset // groups, vector] = turned_ref[pl.ds(row, rows), :].astype(out.dtype)


def in_order(fits, cols, position, slabs, where):
    at = {owner: place for place, owner in enumerate(sum(where, []))}
    table = jnp.array([[at[f, c] for c in range(cols)] for f in range(fits)])
    chosen = table[(jnp.arange(fits) ^ position[0])[:, None], (jnp.arange(cols) ^ position[1])[None]]
    stack = jnp.concatenate(slabs)[chosen]
    _, _, vectors, rows, width = stack.shape
    return stack.transpose(2, 0, 3, 1, 4).reshape(1, vectors, fits * rows, cols * width)


def contracted(fits, cols, first, rows, position, slabs, where, hole_factor, elec_factor):
    count, outer, inner = elec_factor.shape
    holes = hole_factor.shape[1]
    vectors = slabs[0].shape[1]
    block = next(size for size in (8, 4, 2, 1) if count % size == 0)
    inside = rows % 16 == 0
    if inside:
        blocks, groups, places = fits, first, position
    else:
        blocks, groups, places = 1, 1, jnp.zeros_like(position)
        slabs, where = [in_order(fits, cols, position, slabs, where)], [[(0, 0)]]
    piece = (blocks // groups, vectors, holes // blocks, outer)
    kept, *sent = pl.pallas_call(
        functools.partial(contract, blocks, where),
        in_specs=[pl.BlockSpec(memory_space=pltpu.SMEM)]
        + [pl.BlockSpec(memory_space=pltpu.VMEM)] * len(slabs)
        + [pl.BlockSpec(memory_space=pltpu.HBM)] * 2,
        out_specs=[pl.BlockSpec(memory_space=pltpu.VMEM)] * groups,
        out_shape=[jax.ShapeDtypeStruct(piece, jnp.float32)]
        + [jax.ShapeDtypeStruct(piece, jnp.bfloat16)] * (groups - 1),
        scratch_shapes=[
            pltpu.VMEM((vectors, holes, inner), jnp.bfloat16),
            pltpu.VMEM((vectors, outer, holes), jnp.float32),
            pltpu.VMEM((holes, outer), jnp.float32),
            pltpu.VMEM((count // block, block, holes, holes), jnp.bfloat16),
            pltpu.VMEM((count // block, block, outer, inner), jnp.bfloat16),
            pltpu.SemaphoreType.DMA((2, count // block)),
        ],
        compiler_params=pltpu.CompilerParams(vmem_limit_bytes=51 << 20),
        cost_estimate=pl.CostEstimate(
            flops=2 * vectors * count * holes * outer * (inner + holes),
            bytes_accessed=2 * (hole_factor.size + elec_factor.size),
            transcendentals=0,
        ),
    )(places, *slabs, hole_factor, elec_factor)
    if not inside:
        pieces = kept.reshape(vectors, fits, rows, outer).swapaxes(0, 1)
        pieces = pieces[jnp.arange(fits) ^ position[0]].reshape(fits // first, first, vectors, rows, outer)
        kept = pieces[:, 0]
        sent = [pieces[:, step].astype(jnp.bfloat16) for step in range(1, first)]
    return kept, *sent


def local(fits, cols, trial, hole_factor, elec_factor, hole_energy, elec_energy):
    vectors, rows, _ = trial.shape
    radices = digits_of(fits)

    held, owners = trial[None], [(0, 0)]
    bit = cols // 2
    while bit > 1:
        held = jnp.concatenate([held, swap(held, "col", cols, bit)])
        owners = owners + [(f, c ^ bit) for f, c in owners]
        bit //= 2
    stride = 1
    for radix in radices[:-1]:
        arrived = [swap(held, "fit", fits, step * stride) for step in range(1, radix)]
        held = jnp.concatenate([held, *arrived])
        owners = [(f ^ (step * stride), c) for step in range(radix) for f, c in owners]
        stride *= radix
    last = radices[-1] if radices else 1
    position = jnp.stack([lax.axis_index("fit"), lax.axis_index("col")]).astype(jnp.int32)
    chunks = 2 if vectors % 2 == 0 else 1
    size = vectors // chunks
    parts = [held[:, at * size : (at + 1) * size] for at in range(chunks)]
    slabs = []
    for part in parts:
        mine = [part]
        for step in range(1, last):
            mine.append(swap(part, "fit", fits, step * stride))
        slabs.append(mine)
    where = [[(f ^ (step * stride), c) for f, c in owners] for step in range(last)]

    first = radices[0] if radices else 1
    kept, sent = [], []
    for mine in slabs:
        named = where
        if cols > 1:
            mine = mine + [swap(slab, "col", cols, 1) for slab in mine]
            named = where + [[(f, c ^ 1) for f, c in held_by] for held_by in where]
        own, *others = contracted(fits, cols, first, rows, position, mine, named, hole_factor, elec_factor)
        kept.append(own)
        sent.append(others)

    if radices:
        kept = [
            own + sum(swap(other, "fit", fits, step).astype(jnp.float32) for step, other in enumerate(others, 1))
            for own, others in zip(kept, sent)
        ]
    kept = jnp.concatenate(kept, axis=1)
    stride = first
    for radix in radices[1:]:
        split = kept.reshape(kept.shape[0] // radix, radix, *kept.shape[1:])
        kept = split[:, 0]
        for step in range(1, radix):
            kept = kept + swap(split[:, step].astype(jnp.bfloat16), "fit", fits, step * stride).astype(jnp.float32)
        stride *= radix
    spread = elec_energy[None, :] - hole_energy[:, None]
    return kept[0] + spread[None] * trial.astype(jnp.float32)


def solution(mesh):
    in_specs = (
        P(None, "fit", "col"),
        P("fit", None, None),
        P("fit", "col", None),
        P("fit"),
        P("col"),
    )
    fits, cols = mesh.shape["fit"], mesh.shape["col"]

    def body(*args):
        return local(fits, cols, *args)

    return jax.shard_map(body, mesh=mesh, in_specs=in_specs, out_specs=P(None, "fit", "col"), check_vma=False)
```
